32 devices in a mesh: groups: 2 (over x), tm: 16 (over z, y, core).
Axes of the slice: x: 2, y: 2, z: 4, core: 2. Of those that a mesh axis runs over, the one named last changes fastest.
Arguments:
- frames: bfloat16 [8192, 1536], P(('groups', 'tm')), parts along dimension 0, may hold values from -6 to 6
- frame_count: int32 [32], P(('groups', 'tm')), parts along dimension 0, may hold values from 128 to 256, as said below
- lookback_mask: int32 [32, 4], P(('groups', 'tm')), parts along dimension 0, may hold values 0 or 1
- attn_gain: float32 [1536], replicated, may hold values from 0.1 to 1.9
- w_query: bfloat16 [1536, 768], P('tm')
- w_key: bfloat16 [1536, 768], P('tm')
- w_value: bfloat16 [1536, 768], P('tm'), may hold values from -0.15625 to 0.15625
- w_out: bfloat16 [768, 1536], P('tm'), may hold values from -0.21875 to 0.21875
- conv_gain: float32 [1536], replicated, may hold values from 0.1 to 1.9
- w_glu: bfloat16 [1536, 2048], P('tm'), may hold values from -0.15625 to 0.15625
- depthwise: float32 [31, 1024], replicated, may hold values from -1 to 1
- conv_scale: float32 [1024], replicated, may hold values from 0.5 to 2
- conv_shift: float32 [1024], replicated, may hold values from -3 to 3
- w_proj: bfloat16 [1024, 1536], P('tm'), may hold values from -0.1875 to 0.1875
Outputs:
- block_out: bfloat16 [8192, 1536], P(('groups', 'tm')), parts along dimension 0
The draws below stay inside these ranges and needn't reach their ends.
There are 2 independent parts, one for each index of `groups`. The reference program is written for one: setup_inputs(seed, part) draws one part's arguments, and reference() takes and returns one part's arrays. A program takes and returns all parts, laid end to end along the dimension named above; an argument that names none is the same for every part. Nothing has to cross between parts.
Inputs may be any that keep to these rules, and one draw needn't show every extreme that they name: `frame_count`: live frames of each span; the rest of its 256 frames are padding.
All inputs are finite; a program needn't handle non-finite values. No bound on the sum of `lookback_mask` on one device may be relied on, other than what follows from the above.
Results may differ from the reference program's by a relative error of at most 0.0095.
Values may be sent and summed in bfloat16 or wider, within the bound.
No kernel may reach another device: no remote copies, remote signals or barrier semaphores. Data moves between devices by JAX's collectives and lax.ppermute only.
A program may use at most 128 MiB of HBM per device.

```python
import math
import jax
import jax.numpy as jnp
from jax import lax

D = 1536
HEADS = 8
HEAD_DIM = 96
CONV_CH = 1024
KERNEL = 31
FRAMES_DEV = 256
QKV = 768
SPANS = 16
FRAMES = 4096


def paired_weights(key):
    base_query = jax.random.normal(jax.random.fold_in(key, 11), (D, QKV), jnp.float32) * D ** (-0.5)
    base_key = jax.random.normal(jax.random.fold_in(key, 12), (D, QKV), jnp.float32) * D ** (-0.5)
    return (base_query, base_key)


def draw_w_query(key, part):
    return paired_weights(key)[0].astype(jnp.bfloat16)


def draw_w_key(key, part):
    return paired_weights(key)[1].astype(jnp.bfloat16)


def draw_frame_count(key, part):
    counts = jax.random.randint(jax.random.fold_in(key, 21), (SPANS,), FRAMES_DEV // 2, FRAMES_DEV + 1)
    fullest = jax.random.randint(jax.random.fold_in(key, 22), (), 0, SPANS)
    emptiest = (fullest + 1 + jax.random.randint(jax.random.fold_in(key, 23), (), 0, SPANS - 1)) % SPANS
    index = jnp.arange(SPANS)
    counts = jnp.where(index == fullest, FRAMES_DEV, jnp.where(index == emptiest, FRAMES_DEV // 2, counts))
    return counts.astype(jnp.int32)


def set_ends(values, key, least, largest):
    spot = [jax.random.randint(jax.random.fold_in(key, axis), (), 0, length) for axis, length in enumerate(values.shape)]
    longest = values.shape.index(max(values.shape))
    neighbour = spot[:longest] + [(spot[longest] + 1) % values.shape[longest]] + spot[longest + 1:]
    return values.at[tuple(spot)].set(least).at[tuple(neighbour)].set(largest)


def block_levels(stream_key, dims, pieces, least, largest):
    def one(dim, parts):
        heights = jax.random.uniform(jax.random.fold_in(jax.random.fold_in(stream_key, 6), dim), (parts,), jnp.float32, least / len(pieces), largest / len(pieces))
        return jnp.repeat(jnp.exp(heights), dims[dim] // parts).reshape((-1,) + (1,) * (len(dims) - dim - 1))

    level = one(*pieces[0])
    for cut in pieces[1:]:
        level = level * one(*cut)
    return level


def scatter_about(own_key, extent, scale, most, pieces=(), kind=jnp.bfloat16):
    entries = scale * jax.random.normal(own_key, extent, jnp.float32)
    if pieces:
        entries = entries * block_levels(own_key, extent, pieces, -0.22, 0.18)
    return jnp.clip(entries, -most, most).astype(kind)


def setup_inputs(seed: int = 0, part: int = 0) -> dict:
    key_list = jax.random.split(jax.random.key(seed), 15)
    part_keys = jax.random.split(jax.random.fold_in(key_list[14], part), 15)
    frames = scatter_about(part_keys[0], (FRAMES, D), 1.0, 6.0, ((0, 16),))
    frame_count = draw_frame_count(jax.random.fold_in(jax.random.fold_in(key_list[14], part), 71), part)
    lookback_mask = set_ends((jax.random.randint(part_keys[2], (SPANS, 4), 0, 4) < 3).astype(jnp.int32), jax.random.fold_in(part_keys[2], 1), 0, 1)
    attn_gain = jnp.clip(1.0 + 0.18 * jax.random.normal(key_list[3], (D,), jnp.float32), 0.1, 1.9)
    w_query = draw_w_query(jax.random.fold_in(key_list[14], 71), part)
    w_key = draw_w_key(jax.random.fold_in(key_list[14], 71), part)
    w_value = scatter_about(key_list[6], (D, QKV), D ** -0.5, 0.15625, ((0, 16),))
    w_out = scatter_about(key_list[7], (QKV, D), QKV ** -0.5, 0.21875, ((0, 16),))
    conv_gain = jnp.clip(1.0 + 0.18 * jax.random.normal(key_list[8], (D,), jnp.float32), 0.1, 1.9)
    w_glu = scatter_about(key_list[9], (D, 2 * CONV_CH), D ** -0.5, 0.15625, ((0, 16),))
    depthwise = scatter_about(key_list[10], (KERNEL, CONV_CH), KERNEL ** -0.5, 1.0, (), jnp.float32)
    conv_scale = jnp.clip(jnp.exp(jax.random.uniform(key_list[11], (CONV_CH,), jnp.float32, math.log(0.5), math.log(2.0))), 0.5, 2.0)
    conv_shift = scatter_about(key_list[12], (CONV_CH,), 0.5, 3.0, (), jnp.float32)
    w_proj = scatter_about(key_list[13], (CONV_CH, D), CONV_CH ** -0.5, 0.1875, ((0, 16),))
    return dict(frames=frames, frame_count=frame_count, lookback_mask=lookback_mask, attn_gain=attn_gain, w_query=w_query, w_key=w_key, w_value=w_value, w_out=w_out, conv_gain=conv_gain, w_glu=w_glu, depthwise=depthwise, conv_scale=conv_scale, conv_shift=conv_shift, w_proj=w_proj)


def normalize(x, gain):
    xf = x.astype(jnp.float32)
    mean = lax.optimization_barrier(jnp.mean(xf, axis=-1, keepdims=True))
    centered = xf - mean
    var = lax.optimization_barrier(jnp.mean(centered * centered, axis=-1, keepdims=True))
    return (centered * lax.rsqrt(var + 1e-05) * gain).astype(jnp.bfloat16)

def attend(query_c, keys, values, counts, allowed):
    width = query_c.shape[0]
    pos = jnp.arange(3 * width, dtype=jnp.int32)
    section = pos // width
    place = pos % width
    limit = jnp.where(section == 0, counts[0], jnp.where(section == 1, counts[1], counts[2]))
    block = pos // (width // 2)
    allow = lax.optimization_barrier(jnp.sum((block[:, None] == jnp.arange(4, dtype=jnp.int32)[None, :]) * allowed[None, :], axis=1)) + (block >= 4)
    visible = (place < limit) & (allow > 0)
    factor = 1.0 / math.sqrt(HEAD_DIM)

    def one_head(head):
        start = head * HEAD_DIM
        q_head = lax.dynamic_slice_in_dim(query_c, start, HEAD_DIM, 1)
        k_head = lax.dynamic_slice_in_dim(keys, start, HEAD_DIM, 1)
        v_head = lax.dynamic_slice_in_dim(values, start, HEAD_DIM, 1)
        scores = lax.dot_general(q_head, k_head, (((1,), (1,)), ((), ())), preferred_element_type=jnp.float32) * factor
        scores = jnp.where(visible[None, :], scores, -jnp.inf)
        top = lax.optimization_barrier(jnp.max(scores, axis=1, keepdims=True))
        expo = jnp.exp(scores - top)
        weights = (expo / lax.optimization_barrier(jnp.sum(expo, axis=1, keepdims=True))).astype(jnp.bfloat16)
        return jnp.dot(weights, v_head, preferred_element_type=jnp.float32).astype(jnp.bfloat16)
    stacked = lax.map(one_head, jnp.arange(HEADS, dtype=jnp.int32))
    return jnp.transpose(stacked, (1, 0, 2)).reshape(width, HEADS * HEAD_DIM)

def reference(frames, frame_count, lookback_mask, attn_gain, w_query, w_key, w_value, w_out, conv_gain, w_glu, depthwise, conv_scale, conv_shift, w_proj):
    width = FRAMES_DEV
    norm_a = normalize(frames, attn_gain)
    query = jnp.dot(norm_a, w_query, preferred_element_type=jnp.float32).astype(jnp.bfloat16)
    key = jnp.dot(norm_a, w_key, preferred_element_type=jnp.float32).astype(jnp.bfloat16)
    value = jnp.dot(norm_a, w_value, preferred_element_type=jnp.float32).astype(jnp.bfloat16)
    key_pad = jnp.concatenate([jnp.zeros((2 * width, QKV), jnp.bfloat16), key], axis=0)
    value_pad = jnp.concatenate([jnp.zeros((2 * width, QKV), jnp.bfloat16), value], axis=0)
    count_pad = jnp.concatenate([jnp.zeros((2,), jnp.int32), frame_count.astype(jnp.int32)])

    def span(index):
        start = (index * width).astype(jnp.int32)
        query_c = lax.dynamic_slice_in_dim(query, start, width, 0)
        keys = lax.dynamic_slice_in_dim(key_pad, start, 3 * width, 0)
        values = lax.dynamic_slice_in_dim(value_pad, start, 3 * width, 0)
        counts = lax.dynamic_slice_in_dim(count_pad, index.astype(jnp.int32), 3, 0)
        allowed = lax.dynamic_slice_in_dim(lookback_mask, index.astype(jnp.int32), 1, 0)[0]
        return attend(query_c, keys, values, counts, allowed)
    context = lax.map(span, jnp.arange(SPANS, dtype=jnp.int32)).reshape(FRAMES, QKV)
    mid = (frames.astype(jnp.float32) + jnp.dot(context, w_out, preferred_element_type=jnp.float32)).astype(jnp.bfloat16)
    norm_c = normalize(mid, conv_gain)
    glu_in = jnp.dot(norm_c, w_glu, preferred_element_type=jnp.float32)
    position = jnp.arange(FRAMES, dtype=jnp.int32)
    live = position % width < frame_count[position // width]
    gated = jnp.where(live[:, None], glu_in[:, :CONV_CH] * jax.nn.sigmoid(glu_in[:, CONV_CH:]), 0.0).astype(jnp.bfloat16)
    half = KERNEL // 2
    padded = jnp.pad(gated, ((half, half), (0, 0)))
    conv = jnp.zeros((FRAMES, CONV_CH), jnp.float32)
    for tap in range(KERNEL):
        conv = conv + depthwise[tap] * padded[tap:tap + FRAMES].astype(jnp.float32)
    activated = jax.nn.silu(conv * conv_scale + conv_shift).astype(jnp.bfloat16)
    return (mid.astype(jnp.float32) + jnp.dot(activated, w_proj, preferred_element_type=jnp.float32)).astype(jnp.bfloat16)
```

```python
import functools
import math

import jax
import jax.numpy as jnp
from jax import lax
from jax.experimental import pallas as pl
from jax.experimental.pallas import tpu as pltpu
from jax.sharding import PartitionSpec as P

HEADS = 8
HEAD_DIM = 96
KERNEL = 31
HALO = 16
BLOCK = 512
bf16, f32 = jnp.bfloat16, jnp.float32
VMEM = pl.BlockSpec(memory_space=pltpu.VMEM)
ANY = pl.BlockSpec(memory_space=pl.ANY)
SMEM = pl.BlockSpec(memory_space=pltpu.SMEM)
PARAMS = pltpu.CompilerParams(vmem_limit_bytes=56 << 20)


def norm_rows(xf, gain):
    mean = jnp.mean(xf, axis=-1, keepdims=True)
    centered = xf - mean
    var = jnp.mean(centered * centered, axis=-1, keepdims=True)
    return (centered * lax.rsqrt(var + 1e-05) * gain).astype(bf16)


def norm_kernel(info, own, sib, prev, prev_sib, gain, out):
    width = out.shape[1]
    core = info[0]
    rows = 64
    gains = gain[...]
    for ref, slot in ((prev, core), (prev_sib, 1 - core), (own, 2 + core), (sib, 3 - core)):

        def step(i, carry, ref=ref, slot=slot):
            part = ref[pl.ds(pl.multiple_of(i * rows, rows), rows), :].astype(f32)
            out[slot, pl.ds(pl.multiple_of(i * rows, rows), rows), :] = norm_rows(part, gains)
            return carry

        lax.fori_loop(0, width // rows, step, 0)


def attend_kernel(n_pieces, info, meta, norm, *refs):
    pieces = refs[:n_pieces]
    keep, send, weight, q_s, k_s, v_s, sems = refs[n_pieces:]
    width = keep.shape[0]
    cols = keep.shape[1]
    depth = weight.shape[0]
    rows = depth // n_pieces
    core = info[0]
    copies = []
    for i, piece in enumerate(pieces):
        at = pl.multiple_of(info[8 + i] * rows, 16)
        copies.append(pltpu.make_async_copy(piece, weight.at[pl.ds(at, rows), :], sems.at[i]))
    for copy in copies:
        copy.start()
    for copy in copies:
        copy.wait()

    for span in range(4):
        x = norm[span]
        kv = jnp.dot(x, weight[:, cols:], preferred_element_type=f32)
        k_s[span * width : (span + 1) * width, :] = kv[:, :cols].astype(bf16)
        v_s[span * width : (span + 1) * width, :] = kv[:, cols:].astype(bf16)
        if span >= 2:
            q = jnp.dot(x, weight[:, :cols], preferred_element_type=f32)
            q_s[(span - 2) * width : (span - 1) * width, :] = q.astype(bf16)

    pos = lax.broadcasted_iota(jnp.int32, (1, 3 * width), 1)
    factor = 1.0 / math.sqrt(HEAD_DIM)
    for span in range(2):
        section = pos // width
        limit = jnp.where(
            section == 0, meta[span, 0], jnp.where(section == 1, meta[span + 1, 0], meta[span + 2, 0])
        )
        block = pos // (width // 2)
        allow = (block >= 4).astype(jnp.int32)
        for j in range(4):
            allow = allow + jnp.where(block == j, meta[span + 2, 1 + j], 0)
        visible = (pos % width < limit) & (allow > 0)
        bias = jnp.where(visible, 0.0, -jnp.inf)
        tiles = [None] * (cols // 128)
        for head in range(cols // HEAD_DIM):
            lo, hi = head * HEAD_DIM, (head + 1) * HEAD_DIM
            first, last = lo // 128, (hi - 1) // 128
            a, b = first * 128, (last + 1) * 128
            lane = lax.broadcasted_iota(jnp.int32, (1, b - a), 1) + a
            inside = (lane >= lo) & (lane < hi)
            q = q_s[span * width : (span + 1) * width, a:b]
            q = jnp.where(inside, q, jnp.zeros_like(q))
            k = k_s[span * width : (span + 3) * width, a:b]
            scores = lax.dot_general(q, k, (((1,), (1,)), ((), ())), preferred_element_type=f32)
            scores = scores * factor + bias
            top = jnp.max(scores, axis=1, keepdims=True)
            expo = jnp.exp(scores - top)
            total = jnp.sum(expo, axis=1, keepdims=True)
            weights = (expo * (1.0 / total)).astype(bf16)
            v = v_s[span * width : (span + 3) * width, a:b]
            part = jnp.dot(weights, v, preferred_element_type=f32)
            part = jnp.where(inside, part, 0.0)
            for tile in range(first, last + 1):
                piece = part[:, (tile - first) * 128 : (tile - first + 1) * 128]
                tiles[tile] = piece if tiles[tile] is None else tiles[tile] + piece
        context = jnp.concatenate(tiles, axis=1).astype(bf16)

        @pl.when(core == span)
        def _():
            keep[...] = context

        @pl.when(core != span)
        def _():
            send[...] = context


def stack_copies(source, base, rows, scratch, sems, at):
    copies = []
    blocks = scratch.shape[-1] // BLOCK
    for b in range(blocks):
        copies.append(
            pltpu.make_async_copy(
                source.at[:, pl.ds(base + b * rows, rows), :],
                scratch.at[:, :, pl.ds(b * BLOCK, BLOCK)],
                sems.at[at + b],
            )
        )
    return copies


def glu_kernel(packed, info, frames, ctx_own, ctx_sib, gain, *refs):
    if packed:
        slab, mid, gated, first, last, w_out, w_glu, sems = refs
        r_out, r_glu = w_out.shape[1], w_glu.shape[1]
        out_copies = stack_copies(slab, 0, r_out, w_out, sems, 0)
        n_out = len(out_copies)
        glu_copies = stack_copies(slab, n_out * r_out, r_glu, w_glu, sems, n_out)
    else:
        a, b, mid, gated, first, last, w_out, w_glu, sems = refs
        out_copies = [pltpu.make_async_copy(a, w_out.at[0], sems.at[0])]
        glu_copies = [pltpu.make_async_copy(b, w_glu.at[0], sems.at[1])]
    for copy in out_copies + glu_copies:
        copy.start()
    core = info[0]
    own, sib = ctx_own[...], ctx_sib[...]
    low = jnp.where(core == 0, own, sib)
    high = jnp.where(core == 0, sib, own)
    ctx = jnp.concatenate([low, high], axis=1)
    for copy in out_copies:
        copy.wait()
    wo = w_out[...].reshape(-1, w_out.shape[-1])
    total = frames[...].astype(f32) + jnp.dot(ctx, wo, preferred_element_type=f32)
    mids = total.astype(bf16)
    mid[...] = mids
    normed = norm_rows(mids.astype(f32), gain[...])
    for copy in glu_copies:
        copy.wait()
    channels = gated.shape[1]
    width = gated.shape[0]
    live = lax.broadcasted_iota(jnp.int32, (width, 1), 0) < info[1]
    step = 256
    for j in range(channels // step):
        wv = w_glu[:, :, j * step : (j + 1) * step].reshape(-1, step)
        wg = w_glu[:, :, channels + j * step : channels + (j + 1) * step].reshape(-1, step)
        value = jnp.dot(normed, wv, preferred_element_type=f32)
        gate = jnp.dot(normed, wg, preferred_element_type=f32)
        result = jnp.where(live, value * jax.nn.sigmoid(gate), 0.0).astype(bf16)
        gated[:, j * step : (j + 1) * step] = result
        first[:, j * step : (j + 1) * step] = result[:HALO]
        last[:, j * step : (j + 1) * step] = result[width - HALO :]


def conv_kernel(packed, info, gated, before, after, mid, taps, scale, shift, *refs):
    if packed:
        slab, out, w_proj, padded, act, sems = refs
        r_proj = w_proj.shape[1]
        base = slab.shape[1] - r_proj * (w_proj.shape[-1] // BLOCK)
        copies = stack_copies(slab, base, r_proj, w_proj, sems, 0)
    else:
        a, out, w_proj, padded, act, sems = refs
        copies = [pltpu.make_async_copy(a, w_proj.at[0], sems.at[0])]
    for copy in copies:
        copy.start()
    width, channels = gated.shape
    padded[:HALO, :] = jnp.where(info[2] > 0, before[...].astype(f32), 0.0)
    padded[HALO : HALO + width, :] = gated[...].astype(f32)
    padded[HALO + width :, :] = jnp.where(info[3] > 0, after[...].astype(f32), 0.0)
    lanes = 128
    rows = 128
    for cb in range(channels // lanes):
        ch = slice(cb * lanes, (cb + 1) * lanes)
        for rb in range(width // rows):
            acc = jnp.zeros((rows, lanes), f32)
            for r in range(8):
                extent = rows + 24
                view = padded[rb * rows + r : rb * rows + r + extent, ch]
                for a in range(4):
                    tap = 8 * a + r - 1
                    if 0 <= tap < KERNEL:
                        acc = acc + taps[tap : tap + 1, ch] * view[8 * a : 8 * a + rows]
            pre = acc * scale[:, ch] + shift[:, ch]
            act[rb * rows : (rb + 1) * rows, ch] = (pre * jax.nn.sigmoid(pre)).astype(bf16)
    for copy in copies:
        copy.wait()
    wp = w_proj[...].reshape(-1, w_proj.shape[-1])
    total = mid[...].astype(f32) + jnp.dot(act[...], wp, preferred_element_type=f32)
    out[...] = total.astype(bf16)


def blocks_of(w):
    return [w[:, i : i + BLOCK] for i in range(0, w.shape[1], BLOCK)]


def shards(
    frames,
    frame_count,
    lookback_mask,
    attn_gain,
    w_query,
    w_key,
    w_value,
    w_out,
    conv_gain,
    w_glu,
    depthwise,
    conv_scale,
    conv_shift,
    w_proj,
):
    n_groups, n_tm = lax.axis_size("groups"), lax.axis_size("tm")
    group, place = lax.axis_index("groups"), lax.axis_index("tm")
    width, model = frames.shape
    qkv = w_query.shape[1]
    half_qkv = qkv // 2
    channels = w_proj.shape[0] * n_tm
    core = place % 2
    axes = ("groups", "tm")
    everyone = [(g, t) for g in range(n_groups) for t in range(n_tm)]

    def move(x, target, name):
        pairs = []
        for g, t in everyone:
            h, u = target(g, t)
            pairs.append((g * n_tm + t, h * n_tm + u % n_tm))
        with jax.named_scope(name):
            return lax.ppermute(x, axes, pairs)

    swap = functools.partial(move, target=lambda g, t: (g, t ^ 1))
    ring = n_groups == 2 and n_tm == 16

    with jax.named_scope("meta"):
        numbers = jnp.concatenate([frame_count, lookback_mask[0]])
        numbers = jnp.zeros((8, 128), bf16).at[0, :5].set(numbers.astype(bf16))

    if ring:
        with jax.named_scope("pack"):
            slab = jnp.concatenate(blocks_of(w_out) + blocks_of(w_glu) + blocks_of(w_proj), axis=0)
        gathered = lax.all_gather(slab, "tm", axis=0)

        def heads(which):
            parts = [
                lax.dynamic_slice_in_dim(w, which * half_qkv, half_qkv, 1)
                for w in (w_query, w_key, w_value)
            ]
            return jnp.concatenate(parts, axis=1)

        stay, leave = heads(core), heads(1 - core)
        come = swap(leave, name="qs")
        mine = jnp.where(group == 0, stay, come)
        other = jnp.where(group == 0, come, stay)
        mine_par = jnp.where(group == 0, core, 1 - core)
        z, y = place // 4, (place // 2) % 2
        pieces, slots = [mine, other], []
        slots.append((place // 2) * 2 + mine_par)
        slots.append((place // 2) * 2 + 1 - mine_par)
        column = mine
        for k in range(4):
            if k:
                column = move(column, lambda g, t: (g, t + 4), f"qz{k}")
            across = move(column, lambda g, t: (g, t ^ 2), f"qy{k}")
            site = ((z + 4 - k) % 4) * 2 + y
            site_y = ((z + 4 - k) % 4) * 2 + 1 - y
            if k:
                twin = move(column, lambda g, t: (1 - g, t), f"qa{k}")
                pieces += [column, twin]
                slots += [site * 2 + mine_par, site * 2 + 1 - mine_par]
            twin = move(across, lambda g, t: (1 - g, t), f"qb{k}")
            pieces += [across, twin]
            slots += [site_y * 2 + mine_par, site_y * 2 + 1 - mine_par]
    else:
        full = [
            lax.all_gather(w, "tm", axis=0, tiled=True) for w in (w_query, w_key, w_value)
        ]
        parts = [lax.dynamic_slice_in_dim(w, core * half_qkv, half_qkv, 1) for w in full]
        pieces = [jnp.concatenate(parts, axis=1)]
        slots = [jnp.int32(0)]
        fulls = [lax.all_gather(w, "tm", axis=0, tiled=True) for w in (w_out, w_glu, w_proj)]

    prev = move(frames, lambda g, t: (g, t + 2), "fz")
    prev_numbers = move(numbers, lambda g, t: (g, t + 2), "fn")
    sib = swap(frames, name="fs")
    sib_numbers = swap(numbers, name="ns")
    prev_sib = swap(prev, name="fzs")
    prev_sib_numbers = swap(prev_numbers, name="nzs")

    def integers(a):
        return a[0, :5].astype(jnp.int32)

    has_prev = (place >= 2).astype(jnp.int32)
    own_i, sib_i = integers(numbers), integers(sib_numbers)
    prev_i, prev_sib_i = integers(prev_numbers) * has_prev, integers(prev_sib_numbers) * has_prev
    even = core == 0
    meta = jnp.stack(
        [
            jnp.where(even, prev_i, prev_sib_i),
            jnp.where(even, prev_sib_i, prev_i),
            jnp.where(even, own_i, sib_i),
            jnp.where(even, sib_i, own_i),
        ]
    )
    scalars = [core, frame_count[0], (place > 0).astype(jnp.int32), (place < n_tm - 1).astype(jnp.int32)]
    info = jnp.stack([jnp.int32(s) for s in scalars])
    slot_info = jnp.concatenate(
        [info, jnp.zeros((4,), jnp.int32), jnp.stack([jnp.int32(s) for s in slots])]
    )

    norm = pl.pallas_call(
        norm_kernel,
        out_shape=jax.ShapeDtypeStruct((4, width, model), bf16),
        in_specs=[SMEM] + [VMEM] * 5,
        out_specs=VMEM,
        compiler_params=PARAMS,
        name="norm_spans",
    )(info, frames, sib, prev, prev_sib, attn_gain.reshape(1, -1))

    ctx_shape = jax.ShapeDtypeStruct((width, half_qkv), bf16)
    ctx_keep, ctx_send = pl.pallas_call(
        functools.partial(attend_kernel, len(pieces)),
        out_shape=(ctx_shape, ctx_shape),
        in_specs=[SMEM, SMEM, VMEM] + [ANY] * len(pieces),
        out_specs=(VMEM, VMEM),
        scratch_shapes=[
            pltpu.VMEM((model, 3 * half_qkv), bf16),
            pltpu.VMEM((2 * width, half_qkv), bf16),
            pltpu.VMEM((4 * width, half_qkv), bf16),
            pltpu.VMEM((4 * width, half_qkv), bf16),
            pltpu.SemaphoreType.DMA((len(pieces),)),
        ],
        compiler_params=PARAMS,
        name="attend",
    )(slot_info, meta, norm, *pieces)
    ctx_sib = swap(ctx_send, name="cs")

    n_shards = n_tm if ring else 1
    weights = [gathered] if ring else fulls[:2]
    edge = jax.ShapeDtypeStruct((HALO, channels), bf16)
    mid, gated, first, last = pl.pallas_call(
        functools.partial(glu_kernel, ring),
        out_shape=(
            jax.ShapeDtypeStruct((width, model), bf16),
            jax.ShapeDtypeStruct((width, channels), bf16),
            edge,
            edge,
        ),
        in_specs=[SMEM] + [VMEM] * 4 + [ANY] * len(weights),
        out_specs=(VMEM,) * 4,
        scratch_shapes=[
            pltpu.VMEM((n_shards, qkv // n_shards, model), bf16),
            pltpu.VMEM((n_shards, model // n_shards, 2 * channels), bf16),
            pltpu.SemaphoreType.DMA(((model + 2 * channels) // BLOCK,)),
        ],
        compiler_params=PARAMS,
        name="out_glu",
    )(info, frames, ctx_keep, ctx_sib, conv_gain.reshape(1, -1), *weights)

    before = move(last, lambda g, t: (g, t + 1), "hb")
    after = move(first, lambda g, t: (g, t + n_tm - 1), "ha")

    weights = [gathered] if ring else fulls[2:]
    return pl.pallas_call(
        functools.partial(conv_kernel, ring),
        out_shape=jax.ShapeDtypeStruct((width, model), bf16),
        in_specs=[SMEM] + [VMEM] * 7 + [ANY] * len(weights),
        out_specs=VMEM,
        scratch_shapes=[
            pltpu.VMEM((n_shards, channels // n_shards, model), bf16),
            pltpu.VMEM((width + 2 * HALO, channels), f32),
            pltpu.VMEM((width, channels), bf16),
            pltpu.SemaphoreType.DMA((model // BLOCK,)),
        ],
        compiler_params=PARAMS,
        name="conv_proj",
    )(
        info,
        gated,
        before,
        after,
        mid,
        depthwise,
        conv_scale.reshape(1, -1),
        conv_shift.reshape(1, -1),
        *weights,
    )


def solution(mesh):
    return jax.shard_map(
        shards,
        mesh=mesh,
        in_specs=(
            P(("groups", "tm"), None),
            P(("groups", "tm")),
            P(("groups", "tm"), None),
            P(),
            P("tm", None),
            P("tm", None),
            P("tm", None),
            P("tm", None),
            P(),
            P("tm", None),
            P(),
            P(),
            P(),
            P("tm", None),
        ),
        out_specs=P(("groups", "tm"), None),
        check_vma=False,
    )
```

```python
import functools
import math

import jax
import jax.numpy as jnp
from jax import lax
from jax.experimental import pallas as pl
from jax.experimental.pallas import tpu as pltpu
from jax.sharding import PartitionSpec as P

HEAD_DIM = 96
KERNEL = 31
HALO = 16
bf16, f32 = jnp.bfloat16, jnp.float32
VMEM = pl.BlockSpec(memory_space=pltpu.VMEM)
ANY = pl.BlockSpec(memory_space=pl.ANY)
SMEM = pl.BlockSpec(memory_space=pltpu.SMEM)
PARAMS = pltpu.CompilerParams(vmem_limit_bytes=56 << 20)


def core_of():
    return lax.axis_index("tm") % 2


def pick(core, own, sib):
    low = jnp.where(core == 0, own, sib)
    high = jnp.where(core == 0, sib, own)
    return jnp.concatenate([low, high], axis=-1)


def half_of(core, full):
    width = full.shape[-1] // 2
    return jnp.where(core == 0, full[..., :width], full[..., width:])


def norm_rows(xf, gain):
    mean = jnp.mean(xf, axis=-1, keepdims=True)
    centered = xf - mean
    var = jnp.mean(centered * centered, axis=-1, keepdims=True)
    return (centered * lax.rsqrt(var + 1e-05) * gain).astype(bf16)


def slot_of(step, flip_y, flip_parity):
    place = lax.axis_index("tm")
    z, y = place // 4, (place // 2) % 2
    parity = (place % 2 + lax.axis_index("groups") + flip_parity) % 2
    return (((z + 4 - step) % 4) * 2 + (y + flip_y) % 2) * 2 + parity


def fetch(refs, entries, first_row, rows, dst, sems):
    copies = []
    for i, (ref, offset, slot) in enumerate(entries):
        if slot is None:
            copies.append(pltpu.make_async_copy(refs[ref], dst, sems.at[i]))
            continue
        at = pl.multiple_of(slot_of(*slot) * rows, 16)
        copies.append(
            pltpu.make_async_copy(
                refs[ref].at[pl.ds(offset + first_row, rows), :], dst.at[pl.ds(at, rows), :], sems.at[i]
            )
        )
    for copy in copies:
        copy.start()
    return copies


def pack_kernel(count, mask, frames, wq, wk, wv, wo, wg, wp, ext, *refs):
    outs, meta, sems = refs[:-2], refs[-2], refs[-1]
    width = frames.shape[0]
    mixed = (lax.axis_index("tm") + lax.axis_index("groups")) % 2
    copies = []

    def add(a, b):
        copies.append(pltpu.make_async_copy(a, b, sems.at[len(copies)]))
        copies[-1].start()

    def part(w, half, base=0, span=None):
        n = (w.shape[1] if span is None else span) // 2
        return w.at[:, pl.ds(pl.multiple_of(base + half * n, 128), n)], n

    for i, half in enumerate((mixed, 1 - mixed)):
        q, g, oj = outs[3 * i : 3 * i + 3]
        for j, w in enumerate((wq, wk, wv)):
            a, n = part(w, half)
            add(a, q.at[:, pl.ds(j * n, n)])
        channels = wg.shape[1] // 2
        for j in range(2):
            a, n = part(wg, half, j * channels, channels)
            add(a, g.at[:, pl.ds(j * n, n)])
        add(part(wo, half)[0], oj.at[pl.ds(0, wo.shape[0]), :])
        add(part(wp, half)[0], oj.at[pl.ds(wo.shape[0], wp.shape[0]), :])
    add(frames, ext.at[pl.ds(0, width), :])
    lane = lax.broadcasted_iota(jnp.int32, meta.shape, 1)
    values = jnp.where(lane == 0, count[0], 0)
    for j in range(4):
        values = values + jnp.where(lane == 1 + j, mask[0, j], 0)
    meta[...] = values.astype(f32).astype(bf16)
    add(meta, ext.at[pl.ds(width, 16), pl.ds(0, 128)])
    for copy in copies:
        copy.wait()


def meta_kernel(count, mask, frames, ext, meta, sems):
    width = frames.shape[0]
    lane = lax.broadcasted_iota(jnp.int32, meta.shape, 1)
    values = jnp.where(lane == 0, count[0], 0)
    for j in range(4):
        values = values + jnp.where(lane == 1 + j, mask[0, j], 0)
    meta[...] = values.astype(f32).astype(bf16)
    a = pltpu.make_async_copy(frames, ext.at[pl.ds(0, width), :], sems.at[0])
    b = pltpu.make_async_copy(meta, ext.at[pl.ds(width, 16), pl.ds(0, 128)], sems.at[1])
    a.start()
    b.start()
    a.wait()
    b.wait()


def join_kernel(a, b, out, sems):
    n = a.shape[0]
    first = pltpu.make_async_copy(a, out.at[pl.ds(0, n), :], sems.at[0])
    second = pltpu.make_async_copy(b, out.at[pl.ds(n, n), :], sems.at[1])
    first.start()
    second.start()
    first.wait()
    second.wait()


def norm_kernel(own, sib, prev, prev_sib, gain, out, meta):
    width = out.shape[1]
    place = lax.axis_index("tm")
    core = place % 2
    rows = 64
    gains = gain[...]
    for ref, slot, old in (
        (prev, core, True),
        (prev_sib, 1 - core, True),
        (own, 2 + core, False),
        (sib, 3 - core, False),
    ):

        def step(i, carry, ref=ref, slot=slot):
            at = pl.multiple_of(i * rows, rows)
            part = ref[pl.ds(at, rows), :].astype(f32)
            out[slot, pl.ds(at, rows), :] = norm_rows(part, gains)
            return carry

        lax.fori_loop(0, width // rows, step, 0)
        values = ref[width:, :128].astype(f32)
        if old:
            values = jnp.where(place >= 2, values, 0.0)
        meta[slot] = values


def attend_kernel(entries, n_refs, meta, norm, *refs):
    pieces = refs[:n_refs]
    out, weight, q_s, k_s, v_s, sems = refs[n_refs:]
    width, cols = out.shape[1:]
    for copy in fetch(pieces, entries, 0, weight.shape[0] // len(entries), weight, sems):
        copy.wait()

    for span in range(4):
        x = norm[span]
        kv = jnp.dot(x, weight[:, cols:], preferred_element_type=f32)
        k_s[span * width : (span + 1) * width, :] = kv[:, :cols].astype(bf16)
        v_s[span * width : (span + 1) * width, :] = kv[:, cols:].astype(bf16)
        if span >= 2:
            q = jnp.dot(x, weight[:, :cols], preferred_element_type=f32)
            q_s[(span - 2) * width : (span - 1) * width, :] = q.astype(bf16)

    pos = lax.broadcasted_iota(jnp.int32, (1, 3 * width), 1)
    section, block = pos // width, pos // (width // 2)
    in_place = (pos % width).astype(f32)
    factor = 1.0 / math.sqrt(HEAD_DIM)
    for span in range(2):
        limit = jnp.where(
            section == 0,
            meta[span, 0:1, 0:1],
            jnp.where(section == 1, meta[span + 1, 0:1, 0:1], meta[span + 2, 0:1, 0:1]),
        )
        allow = (block >= 4).astype(f32)
        for j in range(4):
            allow = allow + jnp.where(block == j, meta[span + 2, 0:1, 1 + j : 2 + j], 0.0)
        bias = jnp.where((in_place < limit) & (allow > 0.5), 0.0, -jnp.inf)
        tiles = [None] * (cols // 128)
        for head in range(cols // HEAD_DIM):
            lo, hi = head * HEAD_DIM, (head + 1) * HEAD_DIM
            first, last = lo // 128, (hi - 1) // 128
            a, b = first * 128, (last + 1) * 128
            lane = lax.broadcasted_iota(jnp.int32, (1, b - a), 1) + a
            inside = (lane >= lo) & (lane < hi)
            q = q_s[span * width : (span + 1) * width, a:b]
            q = jnp.where(inside, q, jnp.zeros_like(q))
            k = k_s[span * width : (span + 3) * width, a:b]
            scores = lax.dot_general(q, k, (((1,), (1,)), ((), ())), preferred_element_type=f32)
            scores = scores * factor + bias
            top = jnp.max(scores, axis=1, keepdims=True)
            expo = jnp.exp(scores - top)
            total = jnp.sum(expo, axis=1, keepdims=True)
            weights = (expo * (1.0 / total)).astype(bf16)
            v = v_s[span * width : (span + 3) * width, a:b]
            part = jnp.dot(weights, v, preferred_element_type=f32)
            part = jnp.where(inside, part, 0.0)
            for tile in range(first, last + 1):
                piece = part[:, (tile - first) * 128 : (tile - first + 1) * 128]
                tiles[tile] = piece if tiles[tile] is None else tiles[tile] + piece
        out[span] = jnp.concatenate(tiles, axis=1).astype(bf16)


def out_kernel(entries, n_refs, rows, own, sib, ctx, ctx_sib, *refs):
    pieces = refs[:n_refs]
    mid, weight, sems = refs[n_refs:]
    copies = fetch(pieces, entries, 0, rows, weight, sems)
    core = core_of()
    width = mid.shape[1]
    for copy in copies:
        copy.wait()
    for span in range(2):
        context = pick(core, ctx[span], ctx_sib[span])
        total = jnp.dot(context, weight[...], preferred_element_type=f32)
        residual = jnp.where(core == span, half_of(core, own[:width, :]), half_of(core, sib[:width, :]))
        mid[span] = (residual.astype(f32) + total).astype(bf16)


def glu_kernel(entries, n_refs, meta, mid, mid_sib, gain, *refs):
    pieces = refs[:n_refs]
    gated, first, last, weight, sems = refs[n_refs:]
    copies = fetch(pieces, entries, 0, weight.shape[0] // len(entries), weight, sems)
    core = core_of()
    width, channels = gated.shape[1:]
    normed = []
    for span in range(2):
        full = pick(core, mid[span], mid_sib[span]).astype(f32)
        normed.append(norm_rows(full, gain[...]))
    for copy in copies:
        copy.wait()
    place = lax.broadcasted_iota(jnp.int32, (width, 1), 0).astype(f32)
    step = 256
    for j in range(channels // step):
        at = slice(j * step, (j + 1) * step)
        wv = weight[:, at]
        wg = weight[:, channels + j * step : channels + (j + 1) * step]
        for span in range(2):
            value = jnp.dot(normed[span], wv, preferred_element_type=f32)
            gate = jnp.dot(normed[span], wg, preferred_element_type=f32)
            live = place < meta[2 + span, 0:1, 0:1]
            result = jnp.where(live, value * jax.nn.sigmoid(gate), 0.0).astype(bf16)
            gated[span, :, at] = result
            if span == 0:
                first[:, at] = result[:HALO]
            else:
                last[:, at] = result[width - HALO :]


def conv_kernel(chips, gated, before, after, taps, scale, shift, act, padded, tap_s):
    core = core_of()
    chip = lax.axis_index("tm") // 2
    spans, width, channels = gated.shape
    total = spans * width
    padded[:HALO, :] = jnp.where(chip > 0, before[...].astype(f32), 0.0)
    for span in range(spans):
        padded[HALO + span * width : HALO + (span + 1) * width, :] = gated[span].astype(f32)
    padded[HALO + total :, :] = jnp.where(chip < chips - 1, after[...].astype(f32), 0.0)
    tap_s[:KERNEL, :] = half_of(core, taps[...])
    scales, shifts = half_of(core, scale[...]), half_of(core, shift[...])
    lanes = 128
    rows = 128
    for cb in range(channels // lanes):
        ch = slice(cb * lanes, (cb + 1) * lanes)
        for rb in range(total // rows):
            acc = jnp.zeros((rows, lanes), f32)
            for r in range(8):
                extent = rows + 24
                view = padded[rb * rows + r : rb * rows + r + extent, ch]
                for a in range(4):
                    tap = 8 * a + r - 1
                    if 0 <= tap < KERNEL:
                        acc = acc + tap_s[tap : tap + 1, ch] * view[8 * a : 8 * a + rows]
            pre = acc * scales[:, ch] + shifts[:, ch]
            at = (rb * rows) % width
            act[(rb * rows) // width, at : at + rows, ch] = (pre * jax.nn.sigmoid(pre)).astype(bf16)


def proj_kernel(entries, n_refs, rows, skip, act, act_sib, mid, *refs):
    pieces = refs[:n_refs]
    keep, send, weight, sems = refs[n_refs:]
    copies = fetch(pieces, entries, skip, rows, weight, sems)
    core = core_of()
    for copy in copies:
        copy.wait()
    for span in range(2):
        active = pick(core, act[span], act_sib[span])
        total = jnp.dot(active, weight[...], preferred_element_type=f32)
        result = (mid[span].astype(f32) + total).astype(bf16)

        @pl.when(core == span)
        def _(result=result):
            keep[...] = result

        @pl.when(core != span)
        def _(result=result):
            send[...] = result


def join_halves(own, sib, out):
    out[...] = pick(core_of(), own[...], sib[...])


def like(shape, dtype=bf16):
    return jax.ShapeDtypeStruct(shape, dtype)


def call(body, name, out_shape, in_specs, args, scratch=(), out_specs=None):
    single = isinstance(out_shape, jax.ShapeDtypeStruct)
    return pl.pallas_call(
        body,
        out_shape=out_shape,
        in_specs=in_specs,
        out_specs=out_specs if out_specs is not None else (VMEM if single else (VMEM,) * len(out_shape)),
        scratch_shapes=list(scratch),
        compiler_params=PARAMS,
        name=name,
    )(*args)


def dma(n):
    return pltpu.SemaphoreType.DMA((n,))


CLASSES = {"q": "E", "g": "F", "o": "B"}


def shards(
    frames,
    frame_count,
    lookback_mask,
    attn_gain,
    w_query,
    w_key,
    w_value,
    w_out,
    conv_gain,
    w_glu,
    depthwise,
    conv_scale,
    conv_shift,
    w_proj,
):
    n_groups, n_tm = lax.axis_size("groups"), lax.axis_size("tm")
    width, model = frames.shape
    qkv = w_query.shape[1]
    half_qkv, half_model = qkv // 2, model // 2
    channels = w_proj.shape[0] * n_tm
    half_ch = channels // 2
    axes = ("groups", "tm")
    everyone = [(g, t) for g in range(n_groups) for t in range(n_tm)]

    def move(x, target, name):
        pairs = []
        for g, t in everyone:
            h, u = target(g, t)
            pairs.append((g * n_tm + t, h * n_tm + u % n_tm))
        with jax.named_scope(name):
            return lax.ppermute(x, axes, pairs)

    swap = functools.partial(move, target=lambda g, t: (g, t ^ 1))
    ring = n_groups == 2 and n_tm == 16
    ext_shape = like((width + 16, model))

    def route(name, rows, first, second):
        mine = move(first, lambda g, t: (g, t ^ g), f"{name}p")
        other = move(second, lambda g, t: (g, t ^ 1 ^ g), f"{name}r")
        up, cross, twin = (
            lambda g, t: (g, t + 4),
            lambda g, t: (g, t ^ 2),
            lambda g, t: (1 - g, t),
        )
        refs, entries = [], []

        def got(x, step, flip, parity):
            entries.append((len(refs), 0, (step, flip, parity)))
            refs.append(x)

        kind = CLASSES[name]
        if kind == "B":
            both = call(
                join_kernel,
                f"join_{name}",
                like((2 * mine.shape[0], mine.shape[1])),
                [ANY, ANY],
                (mine, other),
                [dma(2)],
                ANY,
            )

            def got_both(x, step, flip):
                for parity in range(2):
                    entries.append((len(refs), parity * mine.shape[0], (step, flip, parity)))
                refs.append(x)

            for k in range(4):
                if k:
                    both = move(both, up, f"{name}z{k}")
                got_both(both, k, 0)
                got_both(move(both, cross, f"{name}y{k}"), k, 1)
            return refs, entries
        for k in range(4):
            if k:
                mine = move(mine, up, f"{name}z{k}")
                if kind == "F":
                    other = move(other, up, f"{name}o{k}")
                else:
                    other = move(mine, twin, f"{name}a{k}")
            got(mine, k, 0, 0)
            got(other, k, 0, 1)
            across = move(mine, cross, f"{name}y{k}")
            got(across, k, 1, 0)
            got(move(across, twin, f"{name}b{k}"), k, 1, 1)
        return refs, entries

    r_model, r_out, r_proj = w_query.shape[0], w_out.shape[0], w_proj.shape[0]
    if ring:
        q_shape, g_shape = like((r_model, 3 * half_qkv)), like((r_model, 2 * half_ch))
        o_shape = like((r_out + r_proj, half_model))
        ext, *sent = call(
            pack_kernel,
            "pack",
            (ext_shape,) + (q_shape, g_shape, o_shape) * 2,
            [SMEM, SMEM] + [ANY] * 7,
            (frame_count, lookback_mask, frames, w_query, w_key, w_value, w_out, w_glu, w_proj),
            [pltpu.VMEM((16, 128), bf16), dma(16)],
            (ANY,) * 7,
        )
        q_refs, q_entries = route("q", r_model, sent[0], sent[3])
        o_refs, o_entries = route("o", r_out, sent[2], sent[5])
        g_refs, g_entries = route("g", r_model, sent[1], sent[4])
        p_refs, p_entries, skip = o_refs, o_entries, r_out
    else:
        ext = call(
            meta_kernel,
            "meta",
            ext_shape,
            [SMEM, SMEM, ANY],
            (frame_count, lookback_mask, frames),
            [pltpu.VMEM((16, 128), bf16), dma(2)],
            ANY,
        )
        core = lax.axis_index("tm") % 2

        def gather(w, pieces=1):
            w = lax.all_gather(w, "tm", axis=0, tiled=True)
            w = w.reshape(w.shape[0], pieces, -1)
            n = w.shape[2] // 2
            return lax.dynamic_slice_in_dim(w, core * n, n, 2).reshape(w.shape[0], pieces * n)

        q_refs = [jnp.concatenate([gather(w) for w in (w_query, w_key, w_value)], axis=1)]
        o_refs, g_refs, p_refs = [gather(w_out)], [gather(w_glu, 2)], [gather(w_proj)]
        q_entries = o_entries = g_entries = p_entries = [(0, 0, None)]
        skip = 0

    prev = move(ext, lambda g, t: (g, t + 2), "fz")
    sib = swap(ext, name="fs")
    prev_sib = swap(prev, name="ft")

    norm, meta = call(
        norm_kernel,
        "norm_spans",
        (like((4, width, model)), like((4, 16, 128), f32)),
        [VMEM] * 5,
        (ext, sib, prev, prev_sib, attn_gain.reshape(1, -1)),
    )
    ctx = call(
        functools.partial(attend_kernel, q_entries, len(q_refs)),
        "attend",
        like((2, width, half_qkv)),
        [VMEM, VMEM] + [ANY] * len(q_refs),
        (meta, norm, *q_refs),
        [
            pltpu.VMEM((model, 3 * half_qkv), bf16),
            pltpu.VMEM((2 * width, half_qkv), bf16),
            pltpu.VMEM((4 * width, half_qkv), bf16),
            pltpu.VMEM((4 * width, half_qkv), bf16),
            dma(len(q_entries)),
        ],
    )
    ctx_sib = swap(ctx, name="cs")
    mid = call(
        functools.partial(out_kernel, o_entries, len(o_refs), r_out),
        "out_proj",
        like((2, width, half_model)),
        [VMEM] * 4 + [ANY] * len(o_refs),
        (ext, sib, ctx, ctx_sib, *o_refs),
        [pltpu.VMEM((qkv, half_model), bf16), dma(len(o_entries))],
    )
    mid_sib = swap(mid, name="ms")
    edge = like((HALO, half_ch))
    gated, first, last = call(
        functools.partial(glu_kernel, g_entries, len(g_refs)),
        "glu",
        (like((2, width, half_ch)), edge, edge),
        [VMEM] * 4 + [ANY] * len(g_refs),
        (meta, mid, mid_sib, conv_gain.reshape(1, -1), *g_refs),
        [pltpu.VMEM((model, 2 * half_ch), bf16), dma(len(g_entries))],
    )
    before = move(last, lambda g, t: (g, t + 2), "hb")
    after = move(first, lambda g, t: (g, t + n_tm - 2), "ha")
    act = call(
        functools.partial(conv_kernel, n_tm // 2),
        "conv",
        like((2, width, half_ch)),
        [VMEM] * 6,
        (gated, before, after, depthwise, conv_scale.reshape(1, -1), conv_shift.reshape(1, -1)),
        [pltpu.VMEM((2 * width + 2 * HALO, half_ch), f32), pltpu.VMEM((32, half_ch), f32)],
    )
    act_sib = swap(act, name="as")
    keep, send = call(
        functools.partial(proj_kernel, p_entries, len(p_refs), r_proj, skip),
        "proj",
        (like((width, half_model)),) * 2,
        [VMEM] * 3 + [ANY] * len(p_refs),
        (act, act_sib, mid, *p_refs),
        [pltpu.VMEM((channels, half_model), bf16), dma(len(p_entries))],
    )
    other = swap(send, name="xs")
    return call(join_halves, "join_out", like((width, model)), [VMEM] * 2, (keep, other))


def solution(mesh):
    return jax.shard_map(
        shards,
        mesh=mesh,
        in_specs=(
            P(("groups", "tm"), None),
            P(("groups", "tm")),
            P(("groups", "tm"), None),
            P(),
            P("tm", None),
            P("tm", None),
            P("tm", None),
            P("tm", None),
            P(),
            P("tm", None),
            P(),
            P(),
            P(),
            P("tm", None),
        ),
        out_specs=P(("groups", "tm"), None),
        check_vma=False,
    )
```
